32 devices in a mesh: space: 16 (over z, x, core), mode: 2 (over y).
Axes of the slice: x: 2, y: 2, z: 4, core: 2. Of those that a mesh axis runs over, the one named last changes fastest.
Arguments:
- field: float32 [3, 16, 128, 64, 256], P(None, 'mode', 'space'), may hold values from -6 to 6
- velocity: float32 [128, 64, 256], P('space'), may hold values from 0.1 to 1
- dispersion: float32 [128, 64, 256], P('space'), may hold values from 0.05 to 0.3
- mobility: float32 [3, 8, 16], replicated, may hold values from -0.2 to 0.2
- material: int32 [128, 64, 256], P('space'), may hold values from 0 to 7
- fixed_mask: int32 [128, 64, 256], P('space'), may hold values 0 or 1
Outputs:
- advanced: float32 [3, 16, 128, 64, 256], P(None, 'mode', 'space')
The draws below stay inside these ranges and needn't reach their ends.
All inputs are finite; a program needn't handle non-finite values. No bound on the sum of `fixed_mask` on one device may be relied on, other than what follows from the above.
Results may differ from the reference program's by a relative error of at most 0.0001.
Values sent between devices are 32-bit elements; how exact they have to be, the bound alone decides.
A program may use at most 128 MiB of HBM per device.

```python
import math
import jax
import jax.numpy as jnp
from jax import lax

METALS = 3
MODES = 16
CLASSES = 8
NY = 64
NZ = 256
STEPS = 2
NX = 128


def place_ends(values, own_key, smallest, top_value):
    index_at = [jax.random.randint(jax.random.fold_in(own_key, axis), (), 0, length) for axis, length in enumerate(values.shape)]
    longest = values.shape.index(max(values.shape))
    beside = index_at[:longest] + [(index_at[longest] + 1) % values.shape[longest]] + index_at[longest + 1:]
    return values.at[tuple(index_at)].set(smallest).at[tuple(beside)].set(top_value)


def shard_levels(stream_key, shape, split, smallest, high):
    factor_of, own = 1.0, jax.random.fold_in(stream_key, 6)
    for position, blocks in split:
        steps = jnp.exp(jax.random.uniform(jax.random.fold_in(own, position), (blocks,), jnp.float32, smallest / len(split), high / len(split)))
        factor_of = factor_of * jnp.repeat(steps, shape[position] // blocks).reshape([-1 if axis == position else 1 for axis in range(len(shape))])
    return factor_of


def centred(own_key, extent, scale, limit, pieces=(), held_as=jnp.bfloat16):
    values = scale * jax.random.normal(own_key, extent, jnp.float32)
    if pieces:
        values = values * shard_levels(own_key, extent, pieces, -0.22, 0.18)
    return jnp.clip(values, -limit, limit).astype(held_as)


def setup_inputs(seed: int = 0) -> dict:
    splits = jax.random.split(jax.random.key(seed), 7)
    return {
        "field": centred(splits[0], (METALS, MODES, NX, NY, NZ), 1.0, 6.0, ((1, 2), (2, 16)), jnp.float32),
        "velocity": jnp.clip(jnp.exp(math.log(1.0) - 2.3025851 * jax.random.uniform(splits[1], (NX, NY, NZ), jnp.float32) ** shard_levels(splits[1], (NX, NY, NZ), ((0, 16),), -0.2, 0.2)), 0.1, 1.0),
        "dispersion": jnp.clip(jnp.exp(math.log(0.3) - 1.7917595 * jax.random.uniform(splits[2], (NX, NY, NZ), jnp.float32) ** shard_levels(splits[2], (NX, NY, NZ), ((0, 16),), -0.2, 0.2)), 0.05, 0.3),
        "mobility": jnp.clip(jax.random.uniform(splits[3], (METALS, CLASSES, MODES), jnp.float32, -0.2, 0.2), -0.2, 0.2),
        "material": place_ends(jax.random.randint(splits[4], (NX, NY, NZ), 0, CLASSES), jax.random.fold_in(splits[4], 1), 0, CLASSES - 1).astype(jnp.int32),
        "fixed_mask": place_ends((jax.random.randint(splits[5], (NX, NY, NZ), 0, 8) < 1).astype(jnp.int32), jax.random.fold_in(splits[5], 1), 0, 1),
    }


TIME_STEP = 0.1
MOBILE_BASE = 0.7

def legendre_weight(order):
    return math.comb(2 * order, order) / 4.0 ** order

def triple_table(terms_count):
    entries = []
    for degree_a in range(terms_count):
        slab_values = []
        for degree_b in range(terms_count):
            row_values = []
            for degree_c in range(terms_count):
                degree_sum = degree_a + degree_b + degree_c
                halfsum = degree_sum // 2
                amount = 0.0
                if degree_sum % 2 == 0 and halfsum >= degree_a and (halfsum >= degree_b) and (halfsum >= degree_c):
                    amount = legendre_weight(halfsum - degree_a) * legendre_weight(halfsum - degree_b) * legendre_weight(halfsum - degree_c)
                    amount = amount / legendre_weight(halfsum) / (degree_sum + 1)
                    amount = amount * math.sqrt((2 * degree_a + 1) * (2 * degree_b + 1) * (2 * degree_c + 1))
                row_values.append(amount)
            slab_values.append(row_values)
        entries.append(slab_values)
    return jnp.asarray(entries, jnp.float32)

def operate(values, velocity, dispersion):
    padded = jnp.pad(values, ((0, 0), (2, 2), (1, 1), (1, 1)))
    middle = padded[:, 2:-2, 1:-1, 1:-1]
    left_two = padded[:, :-4, 1:-1, 1:-1]
    left_one = padded[:, 1:-3, 1:-1, 1:-1]
    right_one = padded[:, 3:-1, 1:-1, 1:-1]
    right_two = padded[:, 4:, 1:-1, 1:-1]
    lower_y = padded[:, 2:-2, :-2, 1:-1]
    upper_y = padded[:, 2:-2, 2:, 1:-1]
    lower_z = padded[:, 2:-2, 1:-1, :-2]
    upper_z = padded[:, 2:-2, 1:-1, 2:]
    spread = (16.0 * (left_one + right_one) - (left_two + right_two) - 30.0 * middle) / 12.0
    spread = spread + (lower_y + upper_y) + (lower_z + upper_z) - 4.0 * middle
    carried = (2.0 * right_one + 3.0 * middle - 6.0 * left_one + left_two) / 6.0
    return dispersion * spread - velocity * carried

def reference(field, velocity, dispersion, mobility, material, fixed_mask):
    modes = mobility.shape[2]
    triple = triple_table(modes)
    movable = (1 - fixed_mask).astype(jnp.float32)
    state = field
    for sweep_index in range(STEPS):
        updated = []
        for metal in range(METALS):
            operated = operate(state[metal], velocity, dispersion)
            coeffs = jnp.moveaxis(mobility[metal][material], -1, 0)
            flat = operated.reshape(modes, -1)
            coupled = MOBILE_BASE * flat
            for term in range(modes):
                mixed = jnp.dot(triple[:, :, term], flat, precision=lax.Precision.HIGHEST)
                coupled = coupled + coeffs[term].reshape(1, -1) * mixed
            updated.append(state[metal] + TIME_STEP * movable * coupled.reshape(operated.shape))
        state = jnp.stack(updated)
    return state
```

```python
import functools

import jax
import jax.numpy as jnp
import numpy as np
from jax import lax
from jax.experimental import pallas as pl
from jax.experimental.pallas import tpu as pltpu
from jax.sharding import PartitionSpec as P

STEPS = 2
TIME_STEP = 0.1
MOBILE_BASE = 0.7
TILE = 8


def quadrature(modes):
    pairs = (3 * (modes - 1) + 2) // 4 + 1
    nodes, weights = np.polynomial.legendre.leggauss(2 * pairs)
    nodes, weights = nodes[pairs:], weights[pairs:] / 2
    scale = np.sqrt(2 * np.arange(modes) + 1.0)
    plus = np.polynomial.legendre.legvander(nodes, modes - 1) * scale
    minus = np.polynomial.legendre.legvander(-nodes, modes - 1) * scale
    return plus, minus, weights


def split_rows(matrix):
    big = np.kron(matrix, np.eye(TILE))
    high = big.astype(jnp.bfloat16)
    low = (big - high.astype(np.float64)).astype(jnp.bfloat16)
    return np.concatenate([high, high, low], axis=1)


def tables(modes, mode_count):
    plus, _, weights = quadrature(modes)
    width = modes // mode_count
    out = []
    for q in range(mode_count):
        order = np.concatenate(
            [np.arange(width) + ((q - d) % mode_count) * width for d in range(mode_count)]
        )
        local = plus[:, order]
        back = (local * weights[:, None]).T
        out.append(
            [
                split_rows(local[:, 0::2]),
                split_rows(local[:, 1::2]),
                split_rows(back[0::2]),
                split_rows(back[1::2]),
            ]
        )
    return [np.stack(t) for t in zip(*out)]


def class_table(mobility):
    plus, minus, _ = quadrature(mobility.shape[2])
    both = jnp.asarray(np.concatenate([plus, minus]), jnp.float32)
    value = MOBILE_BASE + jnp.einsum(
        "qk,mck->mqc", both, mobility, precision=lax.Precision.HIGHEST
    )
    parts = []
    for _ in range(3):
        part = lax.reduce_precision(value, 8, 7)
        parts.append(part)
        value = value - part
    eye = jnp.eye(TILE, dtype=jnp.float32)
    wide = [
        (p[:, :, None, :, None] * eye[None, None, :, None, :]).reshape(
            p.shape[0], p.shape[1] * TILE, p.shape[2] * TILE
        )
        for p in parts
    ]
    return jnp.concatenate(wide, axis=2).astype(jnp.bfloat16)


def split3(value):
    high = value.astype(jnp.bfloat16)
    low = (value - high.astype(jnp.float32)).astype(jnp.bfloat16)
    return jnp.concatenate([high, low, high], axis=0)


def dot(a, b):
    return jnp.dot(a, b, preferred_element_type=jnp.float32)


def couple(operated, material, classes, mats):
    fwd_e, fwd_o, back_e, back_o, ctab = mats
    hot = jnp.concatenate(
        [jnp.where(material == c, 1.0, 0.0) for c in range(classes)], axis=0
    ).astype(jnp.bfloat16)
    factor = dot(ctab[...], jnp.concatenate([hot, hot, hot], axis=0))
    even = dot(fwd_e[...], split3(jnp.concatenate(operated[0::2], axis=0)))
    odd = dot(fwd_o[...], split3(jnp.concatenate(operated[1::2], axis=0)))
    half = even.shape[0]
    up = factor[:half] * (even + odd)
    down = factor[half:] * (even - odd)
    parts = (dot(back_e[...], split3(up + down)), dot(back_o[...], split3(up - down)))
    return [
        parts[j % 2][TILE * (j // 2) : TILE * (j // 2 + 1)] for j in range(len(operated))
    ]


def step_kernel(
    n_blocks, n_out, sides, modes, classes, *refs
):
    refs = list(refs)

    def take(count):
        got = refs[:count]
        del refs[:count]
        return got

    blocks = take(n_blocks)
    xlo, xhi, up8, dn8 = take(4)
    vel, dis, mat, mov = take(4)
    mats = take(5)
    if sides:
        near, ysum, vel_e, dis_e, mat_e, mov_e = take(6)
    outs = take(n_out)
    if sides:
        (ext_out,) = take(1)
    scr, sems = take(2)
    planes, rows, nz = vel.shape
    copies = []
    width = modes // n_blocks
    for b, ref in enumerate(blocks):
        copies.append((ref, scr.at[pl.ds(b * width, width), pl.ds(2, planes), pl.ds(TILE, rows)]))
    copies.append((xlo, scr.at[:, pl.ds(0, 2), pl.ds(TILE, rows)]))
    copies.append((xhi, scr.at[:, pl.ds(planes + 2, 2), pl.ds(TILE, rows)]))
    copies.append((up8, scr.at[:, pl.ds(2, planes), pl.ds(0, TILE)]))
    copies.append((dn8, scr.at[:, pl.ds(2, planes), pl.ds(TILE + rows, TILE)]))
    started = [
        pltpu.make_async_copy(src, dst, sems.at[i]) for i, (src, dst) in enumerate(copies)
    ]
    for copy in started:
        copy.start()

    lane = lax.broadcasted_iota(jnp.int32, (TILE, nz), 1)
    first, final = lane == 0, lane == nz - 1

    def z_sum(centre):
        lower = jnp.where(first, 0.0, pltpu.roll(centre, 1, 1))
        upper = jnp.where(final, 0.0, pltpu.roll(centre, nz - 1, 1))
        return lower + upper

    def weights(v, d):
        return (
            d * (-1.0 / 12.0) - v * (1.0 / 6.0),
            d * (16.0 / 12.0) + v,
            d * -6.5 - v * 0.5,
            d * (16.0 / 12.0) - v * (1.0 / 3.0),
            d * (-1.0 / 12.0),
        )

    def operate(w, d, v5, ypair):
        total = d * (ypair + z_sum(v5[2]))
        for a, b in zip(w, v5):
            total = total + a * b
        return total

    if sides:
        for s in range(sides):
            for g in range(planes // TILE):
                at = slice(g * TILE, (g + 1) * TILE)
                d = dis_e[s, at]
                w = weights(vel_e[s, at], d)
                ops = []
                for j in range(modes):
                    v5 = [near[s, j, g * TILE + o : g * TILE + o + TILE] for o in range(5)]
                    ops.append(operate(w, d, v5, ysum[s, j, at]))
                coupled = couple(ops, mat_e[s, at], classes, mats)
                scale = mov_e[s, at]
                for j in range(modes):
                    ext_out[s, j, at] = (
                        near[s, j, g * TILE + 2 : g * TILE + 2 + TILE] + scale * coupled[j]
                    )
    for copy in started:
        copy.wait()

    y_tiles = rows // TILE

    def body(t, carry):
        x = t // y_tiles
        y0 = pl.multiple_of((t % y_tiles) * TILE, TILE)
        here = (x, pl.ds(y0, TILE))
        d = dis[here]
        w = weights(vel[here], d)
        inner = pl.ds(pl.multiple_of(y0 + TILE, TILE), TILE)
        ops = []
        for j in range(modes):
            tall = scr[j, x + 2, pl.ds(y0, 3 * TILE)]
            ypair = tall[TILE - 1 : 2 * TILE - 1] + tall[TILE + 1 : 2 * TILE + 1]
            v5 = [scr[j, x + o, inner] for o in range(5)]
            ops.append(operate(w, d, v5, ypair))
        coupled = couple(ops, mat[here], classes, mats)
        scale = mov[here]
        share = modes // n_out
        for j in range(modes):
            outs[j // share][j % share, x, pl.ds(y0, TILE)] = (
                scr[j, x + 2, inner] + scale * coupled[j]
            )
        return carry

    lax.fori_loop(0, planes * y_tiles, body, 0, unroll=2)


def run_step(blocks, xlo, xhi, up8, dn8, cells, mats, ext, n_out, classes):
    sides = ext[0].shape[0] if ext else 0
    modes = xlo.shape[0]
    planes, rows, nz = cells[0].shape
    any_spec = pl.BlockSpec(memory_space=pl.ANY)
    vmem = pl.BlockSpec(memory_space=pltpu.VMEM)
    operands = [*blocks, xlo, xhi, up8, dn8, *cells, *mats, *ext]
    n_any = len(blocks) + 4
    shapes = [jax.ShapeDtypeStruct((modes // n_out, planes, rows, nz), jnp.float32)] * n_out
    if sides:
        shapes = shapes + [jax.ShapeDtypeStruct((sides, modes, planes, nz), jnp.float32)]
    padded = modes * (planes + 4) * (rows + 2 * TILE) * nz
    return pl.pallas_call(
        functools.partial(step_kernel, len(blocks), n_out, sides, modes, classes),
        out_shape=shapes,
        in_specs=[any_spec] * n_any + [vmem] * (len(operands) - n_any),
        out_specs=[vmem] * len(shapes),
        scratch_shapes=[
            pltpu.VMEM((modes, planes + 4, rows + 2 * TILE, nz), jnp.float32),
            pltpu.SemaphoreType.DMA((n_any,)),
        ],
        compiler_params=pltpu.CompilerParams(vmem_limit_bytes=32 * 1024 * 1024),
        cost_estimate=pl.CostEstimate(
            flops=modes * planes * rows * nz * 2000, bytes_accessed=8 * padded, transcendentals=0
        ),
        name="step_first" if sides else "step_last",
    )(*operands)


def on_device(field, velocity, dispersion, mobility, material, fixed_mask):
    metals, width, planes, ny, nz = field.shape
    modes, classes = mobility.shape[2], mobility.shape[1]
    n = lax.axis_size("mode")
    q = lax.axis_index("mode")
    size = lax.axis_size("space")
    rows = ny // n
    up_perm = [(i, i + 1) for i in range(size - 1)]
    down_perm = [(i + 1, i) for i in range(size - 1)]
    movable = TIME_STEP * (1 - fixed_mask).astype(jnp.float32)

    def shift(d):
        return [(i, (i + d) % n) for i in range(n)]

    def block_rows(array, axis, owner):
        return lax.dynamic_slice_in_dim(array, owner * rows, rows, axis)

    def row(array, axis, index):
        return lax.dynamic_index_in_dim(array, jnp.clip(index, 0, ny - 1), axis, keepdims=False)

    def side_rows(owner):
        signs = [jnp.where(owner == 0, 1, -1)] if n == 2 else [1, -1]
        out = []
        for sign in signs:
            near = owner * rows + jnp.where(sign > 0, rows, -1)
            inside = jnp.where(sign > 0, rows - 1, 0)
            out.append((near, near + sign, inside, (near >= 0) & (near < ny)))
        return out

    def ext_rows(values, owner):
        return jnp.stack(
            [
                jnp.where(
                    valid, jnp.stack([row(values, 2, near), row(values, 2, far)]), 0.0
                )
                for near, far, _, valid in side_rows(owner)
            ]
        )

    def pick_sides(ext):
        if n == 2:
            above = jnp.where(q == 0, 0.0, ext[0])
            below = jnp.where(q == 0, ext[0], 0.0)
        else:
            below, above = ext[0], ext[1]
        above = jnp.pad(above[:, :, None], ((0, 0), (0, 0), (TILE - 1, 0), (0, 0)))
        below = jnp.pad(below[:, :, None], ((0, 0), (0, 0), (0, TILE - 1), (0, 0)))
        return above, below

    def beside(low, high):
        return lax.ppermute(high, "space", up_perm), lax.ppermute(low, "space", down_perm)

    cells = [block_rows(a, 1, q) for a in (velocity, dispersion, material, movable)]
    ext_cells = [
        jnp.stack([row(a, 1, near) for near, _, _, _ in side_rows(q)])
        for a in (velocity, dispersion, material)
    ]
    ext_cells.append(
        jnp.stack([jnp.where(ok, row(movable, 1, near), 0.0) for near, _, _, ok in side_rows(q)])
    )
    base = [
        lax.dynamic_index_in_dim(jnp.asarray(t), q, 0, keepdims=False)
        for t in tables(modes, n)
    ]
    ctabs = class_table(mobility)

    arrived = []
    for m in range(metals):
        exts, blocks = [ext_rows(field[m], q)], [block_rows(field[m], 2, q)]
        for d in range(1, n):
            target = lax.rem(q + d, n)
            exts.append(lax.ppermute(ext_rows(field[m], target), "mode", shift(d)))
            blocks.append(lax.ppermute(block_rows(field[m], 2, target), "mode", shift(d)))
        arrived.append((exts, blocks))

    result = jnp.zeros(field.shape, jnp.float32)
    for m in range(metals):
        exts, blocks = arrived[m]
        mats = base + [ctabs[m]]
        ext = jnp.concatenate(exts, axis=2)
        near, far = ext[:, 0], ext[:, 1]
        near_lo, near_hi = beside(near[:, :, :2], near[:, :, planes - 2 :])
        inside = jnp.stack(
            [
                jnp.concatenate(
                    [lax.dynamic_index_in_dim(b, at, 2, keepdims=False) for b in blocks], axis=0
                )
                for _, _, at, _ in side_rows(q)
            ]
        )
        xlo, xhi = beside(
            jnp.concatenate([b[:, :2] for b in blocks], axis=0),
            jnp.concatenate([b[:, planes - 2 :] for b in blocks], axis=0),
        )
        padded = jnp.concatenate([near_lo, near, near_hi], axis=2)
        state, ext_new = run_step(
            blocks, xlo, xhi, *pick_sides(near), cells, mats,
            [padded, far + inside, *ext_cells], 1, classes,
        )
        xlo, xhi = beside(state[:, :2], state[:, planes - 2 :])
        outs = run_step(
            [state], xlo, xhi, *pick_sides(ext_new), cells, mats, [], n, classes
        )
        zero = jnp.int32(0)
        for d in range(n):
            part = outs[d]
            if d:
                part = lax.ppermute(part, "mode", shift(n - d))
            owner = lax.rem(q + d, n)
            result = lax.dynamic_update_slice(
                result, part[None], (jnp.int32(m), zero, zero, owner * rows, zero)
            )
    return result


def solution(mesh):
    in_specs = (
        P(None, "mode", "space", None, None),
        P("space", None, None),
        P("space", None, None),
        P(),
        P("space", None, None),
        P("space", None, None),
    )
    out_specs = P(None, "mode", "space", None, None)
    return jax.shard_map(
        on_device, mesh=mesh, in_specs=in_specs, out_specs=out_specs, check_vma=False
    )
```

```python
import functools

import jax
import jax.numpy as jnp
import numpy as np
from jax import lax
from jax.experimental import pallas as pl
from jax.experimental.pallas import tpu as pltpu
from jax.sharding import PartitionSpec as P


TIME_STEP = 0.1
MOBILE_BASE = 0.7
TILE = 8


def quadrature(modes):
    pairs = (3 * (modes - 1) + 2) // 4 + 1
    nodes, weights = np.polynomial.legendre.leggauss(2 * pairs)
    nodes, weights = nodes[pairs:], weights[pairs:] / 2
    scale = np.sqrt(2 * np.arange(modes) + 1.0)
    plus = np.polynomial.legendre.legvander(nodes, modes - 1) * scale
    minus = np.polynomial.legendre.legvander(-nodes, modes - 1) * scale
    return plus, minus, weights


def split_rows(matrix):
    big = np.kron(matrix, np.eye(TILE))
    high = big.astype(jnp.bfloat16)
    low = (big - high.astype(np.float64)).astype(jnp.bfloat16)
    return np.concatenate([high, high, low], axis=1)


def tables(modes, mode_count):
    plus, _, weights = quadrature(modes)
    width = modes // mode_count
    out = []
    for q in range(mode_count):
        order = np.concatenate(
            [np.arange(width) + ((q - d) % mode_count) * width for d in range(mode_count)]
        )
        local = plus[:, order]
        back = (local * weights[:, None]).T
        out.append(
            [
                split_rows(local[:, 0::2]),
                split_rows(local[:, 1::2]),
                split_rows(back[0::2]),
                split_rows(back[1::2]),
            ]
        )
    return [np.stack(t) for t in zip(*out)]


def class_table(mobility):
    plus, minus, _ = quadrature(mobility.shape[2])
    both = jnp.asarray(np.concatenate([plus, minus]), jnp.float32)
    value = MOBILE_BASE + jnp.einsum(
        "qk,mck->mqc", both, mobility, precision=lax.Precision.HIGHEST
    )
    parts = []
    for _ in range(3):
        part = lax.reduce_precision(value, 8, 7)
        parts.append(part)
        value = value - part
    eye = jnp.eye(TILE, dtype=jnp.float32)
    wide = [
        (p[:, :, None, :, None] * eye[None, None, :, None, :]).reshape(
            p.shape[0], p.shape[1] * TILE, p.shape[2] * TILE
        )
        for p in parts
    ]
    return jnp.concatenate(wide, axis=2).astype(jnp.bfloat16)


def split3(value):
    high = value.astype(jnp.bfloat16)
    low = (value - high.astype(jnp.float32)).astype(jnp.bfloat16)
    return jnp.concatenate([high, low, high], axis=0)


def dot(a, b):
    return jnp.dot(a, b, preferred_element_type=jnp.float32)


def couple(operated, material, classes, mats):
    fwd_e, fwd_o, back_e, back_o, ctab = mats
    hot = jnp.concatenate(
        [jnp.where(material == c, 1.0, 0.0) for c in range(classes)], axis=0
    ).astype(jnp.bfloat16)
    factor = dot(ctab[...], jnp.concatenate([hot, hot, hot], axis=0))
    even = dot(fwd_e[...], split3(jnp.concatenate(operated[0::2], axis=0)))
    odd = dot(fwd_o[...], split3(jnp.concatenate(operated[1::2], axis=0)))
    half = even.shape[0]
    up = factor[:half] * (even + odd)
    down = factor[half:] * (even - odd)
    parts = (dot(back_e[...], split3(up + down)), dot(back_o[...], split3(up - down)))
    return [
        parts[j % 2][TILE * (j // 2) : TILE * (j // 2 + 1)] for j in range(len(operated))
    ]


def step_kernel(
    n_blocks, n_out, sides, modes, classes, *refs
):
    refs = list(refs)

    def take(count):
        got = refs[:count]
        del refs[:count]
        return got

    blocks = take(n_blocks)
    xlo, xhi, up8, dn8 = take(4)
    vel, dis, mat, mov = take(4)
    mats = take(5)
    if sides:
        near, ysum, vel_e, dis_e, mat_e, mov_e = take(6)
    outs = take(n_out)
    if sides:
        (ext_out,) = take(1)
    scr, sems = take(2)
    planes, rows, nz = vel.shape
    copies = []
    width = modes // n_blocks
    for b, ref in enumerate(blocks):
        copies.append((ref, scr.at[pl.ds(b * width, width), pl.ds(2, planes), pl.ds(TILE, rows)]))
    copies.append((xlo, scr.at[:, pl.ds(0, 2), pl.ds(TILE, rows)]))
    copies.append((xhi, scr.at[:, pl.ds(planes + 2, 2), pl.ds(TILE, rows)]))
    copies.append((up8, scr.at[:, pl.ds(2, planes), pl.ds(0, TILE)]))
    copies.append((dn8, scr.at[:, pl.ds(2, planes), pl.ds(TILE + rows, TILE)]))
    started = [
        pltpu.make_async_copy(src, dst, sems.at[i]) for i, (src, dst) in enumerate(copies)
    ]
    for copy in started:
        copy.start()

    lane = lax.broadcasted_iota(jnp.int32, (TILE, nz), 1)
    first, final = lane == 0, lane == nz - 1

    def z_sum(centre):
        lower = jnp.where(first, 0.0, pltpu.roll(centre, 1, 1))
        upper = jnp.where(final, 0.0, pltpu.roll(centre, nz - 1, 1))
        return lower + upper

    def weights(v, d):
        return (
            d * (-1.0 / 12.0) - v * (1.0 / 6.0),
            d * (16.0 / 12.0) + v,
            d * -6.5 - v * 0.5,
            d * (16.0 / 12.0) - v * (1.0 / 3.0),
            d * (-1.0 / 12.0),
        )

    def operate(w, d, v5, ypair):
        total = d * (ypair + z_sum(v5[2]))
        for a, b in zip(w, v5):
            total = total + a * b
        return total

    if sides:
        for s in range(sides):
            for g in range(planes // TILE):
                at = slice(g * TILE, (g + 1) * TILE)
                d = dis_e[s, at]
                w = weights(vel_e[s, at], d)
                ops = []
                for j in range(modes):
                    v5 = [near[s, j, g * TILE + o : g * TILE + o + TILE] for o in range(5)]
                    ops.append(operate(w, d, v5, ysum[s, j, at]))
                coupled = couple(ops, mat_e[s, at], classes, mats)
                scale = mov_e[s, at]
                for j in range(modes):
                    ext_out[s, j, at] = (
                        near[s, j, g * TILE + 2 : g * TILE + 2 + TILE] + scale * coupled[j]
                    )
    for copy in started:
        copy.wait()

    y_tiles = rows // TILE

    def body(t, carry):
        x = t // y_tiles
        y0 = pl.multiple_of((t % y_tiles) * TILE, TILE)
        here = (x, pl.ds(y0, TILE))
        d = dis[here]
        w = weights(vel[here], d)
        inner = pl.ds(pl.multiple_of(y0 + TILE, TILE), TILE)
        ops = []
        for j in range(modes):
            tall = scr[j, x + 2, pl.ds(y0, 3 * TILE)]
            ypair = tall[TILE - 1 : 2 * TILE - 1] + tall[TILE + 1 : 2 * TILE + 1]
            v5 = [scr[j, x + o, inner] for o in range(5)]
            ops.append(operate(w, d, v5, ypair))
        coupled = couple(ops, mat[here], classes, mats)
        scale = mov[here]
        share = modes // n_out
        for j in range(modes):
            outs[j // share][j % share, x, pl.ds(y0, TILE)] = (
                scr[j, x + 2, inner] + scale * coupled[j]
            )
        return carry

    lax.fori_loop(0, planes * y_tiles, body, 0, unroll=2)


def run_step(blocks, xlo, xhi, up8, dn8, cells, mats, ext, n_out, classes):
    sides = ext[0].shape[0] if ext else 0
    modes = xlo.shape[0]
    planes, rows, nz = cells[0].shape
    any_spec = pl.BlockSpec(memory_space=pl.ANY)
    vmem = pl.BlockSpec(memory_space=pltpu.VMEM)
    operands = [*blocks, xlo, xhi, up8, dn8, *cells, *mats, *ext]
    n_any = len(blocks) + 4
    shapes = [jax.ShapeDtypeStruct((modes // n_out, planes, rows, nz), jnp.float32)] * n_out
    if sides:
        shapes = shapes + [jax.ShapeDtypeStruct((sides, modes, planes, nz), jnp.float32)]
    padded = modes * (planes + 4) * (rows + 2 * TILE) * nz
    return pl.pallas_call(
        functools.partial(step_kernel, len(blocks), n_out, sides, modes, classes),
        out_shape=shapes,
        in_specs=[any_spec] * n_any + [vmem] * (len(operands) - n_any),
        out_specs=[vmem] * len(shapes),
        scratch_shapes=[
            pltpu.VMEM((modes, planes + 4, rows + 2 * TILE, nz), jnp.float32),
            pltpu.SemaphoreType.DMA((n_any,)),
        ],
        compiler_params=pltpu.CompilerParams(vmem_limit_bytes=32 * 1024 * 1024),
        cost_estimate=pl.CostEstimate(
            flops=modes * planes * rows * nz * 2000, bytes_accessed=8 * padded, transcendentals=0
        ),
        name="step_first" if sides else "step_last",
    )(*operands)


def on_device(field, velocity, dispersion, mobility, material, fixed_mask):
    metals, width, planes, ny, nz = field.shape
    modes, classes = mobility.shape[2], mobility.shape[1]
    n = lax.axis_size("mode")
    q = lax.axis_index("mode")
    size = lax.axis_size("space")
    rows = ny // n
    up_perm = [(i, i + 1) for i in range(size - 1)]
    down_perm = [(i + 1, i) for i in range(size - 1)]
    movable = TIME_STEP * (1 - fixed_mask).astype(jnp.float32)

    def shift(d):
        return [(i, (i + d) % n) for i in range(n)]

    def block_rows(array, axis, owner):
        return lax.dynamic_slice_in_dim(array, owner * rows, rows, axis)

    def row(array, axis, index):
        return lax.dynamic_index_in_dim(array, jnp.clip(index, 0, ny - 1), axis, keepdims=False)

    def side_rows(owner):
        signs = [jnp.where(owner == 0, 1, -1)] if n == 2 else [1, -1]
        out = []
        for sign in signs:
            near = owner * rows + jnp.where(sign > 0, rows, -1)
            inside = jnp.where(sign > 0, rows - 1, 0)
            out.append((near, near + sign, inside, (near >= 0) & (near < ny)))
        return out

    def ext_rows(owner):
        return jnp.stack(
            [
                jnp.where(valid, jnp.stack([row(field, 3, near), row(field, 3, far)]), 0.0)
                for near, far, _, valid in side_rows(owner)
            ]
        )

    def field_block(m, owner):
        zero = jnp.int32(0)
        return lax.dynamic_slice(
            field,
            (jnp.int32(m), zero, zero, owner * rows, zero),
            (1, width, planes, rows, nz),
        )[0]

    def pick_sides(ext):
        if n == 2:
            above = jnp.where(q == 0, 0.0, ext[0])
            below = jnp.where(q == 0, ext[0], 0.0)
        else:
            below, above = ext[0], ext[1]
        above = jnp.pad(above[:, :, None], ((0, 0), (0, 0), (TILE - 1, 0), (0, 0)))
        below = jnp.pad(below[:, :, None], ((0, 0), (0, 0), (0, TILE - 1), (0, 0)))
        return above, below

    def beside(low, high):
        before = lax.ppermute(high, "space", up_perm)
        after = lax.ppermute(low, "space", down_perm)
        return before, after

    exts = [lax.ppermute(ext_rows(lax.rem(q + d, n)), "mode", shift(d)) for d in range(1, n)]
    arrived = []
    for m in range(metals):
        blocks = []
        for d in range(1, n):
            piece = field_block(m, lax.rem(q + d, n))
            blocks.append(lax.ppermute(piece, "mode", shift(d)))
        arrived.append([field_block(m, q)] + blocks)

    cells = [block_rows(a, 1, q) for a in (velocity, dispersion, material, movable)]
    ext_cells = [
        jnp.stack([row(a, 1, near) for near, _, _, _ in side_rows(q)])
        for a in (velocity, dispersion, material)
    ]
    ext_cells.append(
        jnp.stack([jnp.where(ok, row(movable, 1, near), 0.0) for near, _, _, ok in side_rows(q)])
    )
    base = [
        lax.dynamic_index_in_dim(jnp.asarray(t), q, 0, keepdims=False)
        for t in tables(modes, n)
    ]
    ctabs = class_table(mobility)

    ext = jnp.concatenate([ext_rows(q)] + exts, axis=3)
    near_all, far_all = ext[:, 0], ext[:, 1]
    near_lo, near_hi = beside(near_all[:, :, :, :2], near_all[:, :, :, planes - 2 :])
    padded_all = jnp.concatenate([near_lo, near_all, near_hi], axis=3)

    zero = jnp.int32(0)

    def finish(m, result, state, again, ext_new):
        outs = run_step(
            [state], *again, *pick_sides(ext_new), cells, base + [ctabs[m]], [], n, classes
        )
        for d in range(n):
            part = outs[d]
            if d:
                part = lax.ppermute(part, "mode", shift(n - d))
            owner = lax.rem(q + d, n)
            result = lax.dynamic_update_slice(
                result, part[None], (jnp.int32(m), zero, zero, owner * rows, zero)
            )
        return result

    result = jnp.zeros(field.shape, jnp.float32)
    for m in range(metals):
        blocks = arrived[m]
        if not m:
            blocks, padded_all = lax.optimization_barrier((blocks, padded_all))
        else:
            blocks, ext_new = lax.optimization_barrier((blocks, ext_new))
            pending = (state, again, ext_new)
        mats = base + [ctabs[m]]
        near, far = near_all[:, m], far_all[:, m]
        inside = jnp.stack(
            [
                jnp.concatenate(
                    [lax.dynamic_index_in_dim(b, at, 2, keepdims=False) for b in blocks], axis=0
                )
                for _, _, at, _ in side_rows(q)
            ]
        )
        xlo, xhi = beside(
            jnp.concatenate([b[:, :2] for b in blocks], axis=0),
            jnp.concatenate([b[:, planes - 2 :] for b in blocks], axis=0),
        )
        if m:
            result = finish(m - 1, result, *pending)
        sides = pick_sides(near)
        state, ext_new = run_step(
            blocks, xlo, xhi, *sides, cells, mats,
            [padded_all[:, m], far + inside, *ext_cells], 1, classes,
        )
        again = beside(state[:, :2], state[:, planes - 2 :])
    result = finish(metals - 1, result, state, again, ext_new)
    return result


def solution(mesh):
    in_specs = (
        P(None, "mode", "space", None, None),
        P("space", None, None),
        P("space", None, None),
        P(),
        P("space", None, None),
        P("space", None, None),
    )
    out_specs = P(None, "mode", "space", None, None)


    return jax.shard_map(
        on_device, mesh=mesh, in_specs=in_specs, out_specs=out_specs, check_vma=False
    )
```
